1024 devices in a mesh: blk: 32 (over z_hi, y), nbr: 32 (over z_lo, x, core).
Axes of the slice: x: 4, y: 8, z: 16 (z_hi: 4, z_lo: 4; z = z_hi * 4 + z_lo), core: 2. Of those that a mesh axis runs over, the one named last changes fastest.
Arguments:
- positions: float32 [3, 524288], P(None, ('blk', 'nbr')), may hold values from -6 to 6
- density: float32 [3, 524288], P(None, ('blk', 'nbr')), may hold values from -1.2 to 1.2
- upsample: float32 [32, 128], replicated, may hold values from -1 to 1
- cell_map: int32 [32, 32], P('blk'), may hold values from 0 to 31, as said below
- near_list: int32 [1024, 124, 2], P(('blk', 'nbr')), may hold values from -1 to 31, as said below
Outputs:
- velocity: float32 [3, 524288], P(None, ('blk', 'nbr'))
The draws below stay inside these ranges and needn't reach their ends.
Inputs may be any that keep to these rules, and one draw needn't show every extreme that they name: Each row of cell_map is a permutation of the nbr indices. In near_list[c] every entry is either (-1, -1) or a pair (k, t) with t a cell id of c's row other than c's own; the pairs of one list are distinct; no cell id is named by more than 4 entries of one list, and in every row one cell is named by exactly 4 entries of every other cell's list.
All inputs are finite; a program needn't handle non-finite values.
Results may differ from the reference program's by a relative error of at most 0.0003.
Values sent between devices are 32-bit elements; how exact they have to be, the bound alone decides.
A program may use at most 32 MiB of HBM per device.

```python
import math
import jax
import jax.numpy as jnp
from jax import lax

P_SIZE = 512
PANELS = 16
SLOTS = 4
PC = 32
PW = 128
CELLS = 1024
NEAR = 124
N_BLK = 32
N_NBR = 32


def near_tables(key):
    map_keys = jax.random.split(jax.random.fold_in(key, 31), N_BLK)
    cell_table = jax.vmap(lambda sub_key: jax.random.permutation(sub_key, N_NBR))(map_keys).astype(jnp.int32)
    hub_cell = jax.random.randint(jax.random.fold_in(key, 32), (N_BLK,), 0, N_NBR)
    levels = jax.random.randint(jax.random.fold_in(key, 33), (N_BLK, N_NBR), 1, 9)
    levels = jnp.where(jnp.arange(N_NBR)[None, :] == hub_cell[:, None], 8, levels)
    return (cell_table, levels)


def draw_cell_map(key, part):
    return near_tables(key)[0]


def draw_near_list(key, part):
    cell_table, levels = near_tables(key)
    own_ids = jnp.argsort(cell_table, axis=1).astype(jnp.int32)
    offsets = jnp.arange(1, N_NBR, dtype=jnp.int32)
    targets = (own_ids[:, :, None] + offsets[None, None, :]) % N_NBR
    total_lists = N_BLK * N_NBR * (N_NBR - 1)
    panel_keys = jax.random.split(jax.random.fold_in(key, 34), total_lists)
    panel_draw = jax.vmap(lambda sub_key: jax.random.permutation(sub_key, PANELS)[:SLOTS])(panel_keys)
    panel_draw = panel_draw.reshape(N_BLK, N_NBR, N_NBR - 1, SLOTS).astype(jnp.int32)
    rolls = jax.random.randint(jax.random.fold_in(key, 35), (N_BLK, N_NBR, N_NBR - 1, SLOTS), 0, 8)
    target_level = levels[jnp.arange(N_BLK)[:, None, None], targets]
    keeping = rolls < target_level[..., None]
    target_full = jnp.broadcast_to(targets[..., None], (N_BLK, N_NBR, N_NBR - 1, SLOTS))
    panel_entry = jnp.where(keeping, panel_draw, -1)
    target_entry = jnp.where(keeping, target_full, -1)
    entries_all = jnp.stack([panel_entry, target_entry], axis=-1).reshape(N_BLK * N_NBR, NEAR, 2)
    order_keys = jax.random.split(jax.random.fold_in(key, 36), N_BLK * N_NBR)
    orders = jax.vmap(lambda sub_key: jax.random.permutation(sub_key, NEAR))(order_keys)
    entries_all = jnp.take_along_axis(entries_all, orders[:, :, None], axis=1)
    return entries_all.astype(jnp.int32)


def shard_levels(own_key, shape, pieces, least, top_value):
    def one(axis_at, blocks):
        draws = jax.random.uniform(jax.random.fold_in(jax.random.fold_in(own_key, 6), axis_at), (blocks,), jnp.float32, least / len(pieces), top_value / len(pieces))
        return jnp.repeat(jnp.exp(draws), shape[axis_at] // blocks).reshape((-1,) + (1,) * (len(shape) - axis_at - 1))

    loudness = one(*pieces[0])
    for cut in pieces[1:]:
        loudness = loudness * one(*cut)
    return loudness


def bell_draw(stream_key, dims, deviation, reach, pieces=(), kind=jnp.bfloat16):
    result = jax.random.normal(stream_key, dims, jnp.float32) * deviation
    if len(pieces) > 0:
        result = shard_levels(stream_key, dims, pieces, -0.22, 0.18) * result
    return jnp.clip(result, min=-reach, max=reach).astype(kind)


def setup_inputs(seed: int = 0) -> dict:
    arg_keys = jax.random.split(jax.random.key(seed), 6)
    positions = bell_draw(arg_keys[0], (3, CELLS * P_SIZE), 1.0, 6.0, ((1, 1024),), jnp.float32)
    density = bell_draw(arg_keys[1], (3, CELLS * P_SIZE), 0.2, 1.2, ((1, 1024),), jnp.float32)
    upsample = bell_draw(arg_keys[2], (PC, PW), PC ** -0.5, 1.0, (), jnp.float32)
    cell_map = draw_cell_map(jax.random.fold_in(arg_keys[5], 71), 0)
    near_list = draw_near_list(jax.random.fold_in(arg_keys[5], 71), 0)
    return {"positions": positions, "density": density, "upsample": upsample, "cell_map": cell_map, "near_list": near_list}


FAR_REG_SQ = 0.0625
NEAR_REG_SQ = 0.01
STOKES_COEF = 1.0 / (8.0 * math.pi)

def stokeslet(targets, sources, densities, reg_sq):
    offset_vec = targets[:, :, None] - sources[:, None, :]
    dist_sq = lax.optimization_barrier(jnp.sum(offset_vec * offset_vec, axis=0)) + reg_sq
    inv_cube = lax.rsqrt(dist_sq) / dist_sq
    leading = (dist_sq + reg_sq) * inv_cube
    projected = lax.optimization_barrier(jnp.sum(offset_vec * densities[:, None, :], axis=0)) * inv_cube
    first = lax.optimization_barrier(jnp.sum(leading[None] * densities[:, None, :], axis=-1))
    second = lax.optimization_barrier(jnp.sum(offset_vec * projected[None], axis=-1))
    return STOKES_COEF * (first + second)

def upsample_panels(panel_data, table):
    raised = jnp.einsum('kcp,pw->kcw', panel_data, table, precision=lax.Precision.HIGHEST)
    ratio = panel_data.shape[2] / table.shape[1]
    return jnp.concatenate([raised[:, :3], raised[:, 3:] * ratio], axis=1)

def reference(positions, density, upsample, cell_map, near_list):
    col_pos = positions.reshape(3, N_BLK, N_NBR, P_SIZE)
    col_den = density.reshape(3, N_BLK, N_NBR, P_SIZE)

    def column_far(column):
        tgt_pos = lax.dynamic_index_in_dim(col_pos, column, 2, keepdims=False)
        tgt_den = lax.dynamic_index_in_dim(col_den, column, 2, keepdims=False)
        targets = tgt_pos.reshape(3, N_BLK * P_SIZE)
        blocks = jnp.transpose(jnp.concatenate([tgt_pos, tgt_den], axis=0), (1, 0, 2))

        def add_block(summed, source_block):
            return (summed + stokeslet(targets, source_block[:3], source_block[3:], FAR_REG_SQ), None)
        summed, _ = lax.scan(add_block, jnp.zeros((3, N_BLK * P_SIZE), jnp.float32), blocks)
        return summed.reshape(3, N_BLK, P_SIZE)
    far_cols = lax.map(column_far, jnp.arange(N_NBR, dtype=jnp.int32))
    far_field = jnp.transpose(far_cols, (1, 2, 0, 3)).reshape(3, CELLS * P_SIZE)
    both = jnp.concatenate([positions, density], axis=0).reshape(6, CELLS, PANELS, PC)
    coarse = jnp.transpose(both, (1, 2, 0, 3)).reshape(CELLS * PANELS, 6, PC)
    fine_all = upsample_panels(coarse, upsample).reshape(CELLS, PANELS, 6, PW)
    lists = near_list.reshape(N_BLK, N_NBR, NEAR, 2)
    panel_ids = lists[..., 0]
    target_ids = lists[..., 1]
    is_valid = target_ids >= 0
    matches = target_ids[..., None] == jnp.arange(N_NBR, dtype=jnp.int32)
    dest_device = lax.optimization_barrier(jnp.sum(jnp.where(matches, cell_map[:, None, None, :], 0), axis=-1)).astype(jnp.int32)
    position = jnp.arange(NEAR, dtype=jnp.int32)
    earlier = (dest_device[..., :, None] == dest_device[..., None, :]) & is_valid[..., :, None] & is_valid[..., None, :] & (position[None, :] < position[:, None])
    rank_in_dest = lax.optimization_barrier(jnp.sum(earlier.astype(jnp.int32), axis=-1))
    slot_id = dest_device * SLOTS + rank_in_dest
    hits = (slot_id[..., None, :] == jnp.arange(N_NBR * SLOTS, dtype=jnp.int32)[:, None]) & is_valid[..., None, :]
    panel_at = lax.optimization_barrier(jnp.sum(jnp.where(hits, panel_ids[..., None, :], 0), axis=-1)).astype(jnp.int32)
    filled = jnp.any(hits, axis=-1)

    def near_cell(cell):
        row = cell // N_NBR
        column = cell % N_NBR
        ids = lax.dynamic_slice(panel_at, (row, jnp.int32(0), column * SLOTS), (1, N_NBR, SLOTS))[0]
        used = lax.dynamic_slice(filled, (row, jnp.int32(0), column * SLOTS), (1, N_NBR, SLOTS))[0]
        src_cells = row * N_NBR + jnp.arange(N_NBR, dtype=jnp.int32)[:, None]
        chosen = fine_all[src_cells, ids]
        chosen = jnp.where(used[:, :, None, None], chosen, jnp.zeros_like(chosen))
        flattened = jnp.transpose(chosen, (2, 0, 1, 3)).reshape(6, N_NBR * SLOTS * PW)
        targets = lax.dynamic_slice_in_dim(positions, cell * P_SIZE, P_SIZE, 1)
        return stokeslet(targets, flattened[:3], flattened[3:], NEAR_REG_SQ)
    near_cells = lax.map(near_cell, jnp.arange(CELLS, dtype=jnp.int32))
    near_field = jnp.transpose(near_cells, (1, 0, 2)).reshape(3, CELLS * P_SIZE)
    return far_field + near_field
```

```python
import functools
import math

import jax
import jax.numpy as jnp
from jax import lax
from jax.experimental import pallas as pl
from jax.experimental.pallas import tpu as pltpu
from jax.sharding import PartitionSpec as P

F32 = jnp.float32
BF16 = jnp.bfloat16
MESH = pl.DeviceIdType.MESH
FAR_REG_SQ = 0.0625
NEAR_REG_SQ = 0.01
STOKES_COEF = 1.0 / (8.0 * math.pi)

PTS = 512
PEERS = 32
ZN = 4
YN = 8
NEAR_BLOCKS = PEERS - 1
FAR0 = NEAR_BLOCKS
BLOCKS = NEAR_BLOCKS + ZN * YN


def split3(a):
    a1 = a.astype(BF16)
    r = a - a1.astype(F32)
    a2 = r.astype(BF16)
    r = r - a2.astype(F32)
    return a1, a2, r.astype(BF16)


def split3f(a):
    a1 = a.astype(BF16).astype(F32)
    r = a - a1
    a2 = r.astype(BF16).astype(F32)
    return a1, a2, r - a2


def pack_kernel(list_ref, map_ref, pos_ref, den_ref, up_ref, own_ref, out_ref, wide_ref, table, count):
    zero = jnp.zeros((1, PTS), F32)
    own = jnp.concatenate([pos_ref[...], zero, den_ref[...], zero], axis=0)
    own_ref[...] = own
    row = lax.broadcasted_iota(jnp.int32, (8, 128), 0)
    scaled = [jnp.where(row < 4, own[:, 128 * v : 128 * v + 128], 0.25 * own[:, 128 * v : 128 * v + 128]) for v in range(4)]
    for v in range(4):
        for r in range(4):
            table[4 * v + r] = scaled[v] if r == 0 else pltpu.roll(scaled[v], 32 * r, 1)
    out_ref[...] = jnp.zeros_like(out_ref)
    up = up_ref[...]
    none = jnp.zeros_like(up)
    for s in range(4):
        wide_ref[32 * s : 32 * s + 32, :] = jnp.concatenate([up if q == s else none for q in range(4)], axis=1)
    lane_slot = lax.broadcasted_iota(jnp.int32, (8, 128), 1) // 32
    for j in range(PEERS + 1):
        count[j] = 0

    def entry(e, carry):
        k = jnp.maximum(list_ref[2 * e], 0)
        t = list_ref[2 * e + 1]
        dest = jnp.where(t >= 0, map_ref[0, jnp.maximum(t, 0)], PEERS)
        slot = jnp.bitwise_and(count[dest], 3)
        count[dest] = slot + 1
        tile = table[4 * (k // 4) + jnp.bitwise_and(slot - k, 3)]
        out_ref[dest] = jnp.where(lane_slot == slot, tile, out_ref[dest])
        return carry

    lax.fori_loop(0, list_ref.shape[0] // 2, entry, 0)


def bc(t, r):
    return jnp.broadcast_to(t[r : r + 1, :], t.shape)


def prepare(t, center, row, ya_ref, w_ref):
    tc = t - center
    g = pltpu.roll(tc, 4, 0)
    sq = tc * tc
    df = tc * g
    nb = jnp.broadcast_to(sq[0:1] + sq[1:2] + sq[2:3], t.shape)
    db = jnp.broadcast_to(df[0:1] + df[1:2] + df[2:3], t.shape)
    s = jnp.where(row < 3, tc, jnp.where(row == 3, nb, jnp.where(row == 4, 1.0, 0.0)))
    s1, s2, s3 = split3f(s)
    ya_ref[...] = jnp.concatenate([s1, s2, s3, s1, s2, s1], axis=0).astype(BF16)
    low = row < 4
    f2 = jnp.where(low, g, tc)
    w1 = jnp.where(low, bc(tc, 0), bc(tc, 1)) * f2
    w2 = jnp.where(low, bc(tc, 2) * g, nb * tc + db * g)
    w1 = jnp.where(row == 3, bc(tc, 4), jnp.where(row == 7, bc(tc, 5), w1))
    w2 = jnp.where(row == 3, bc(tc, 6), w2)
    p1, p2, p3 = split3(jnp.concatenate([w1, w2], axis=0))
    w_ref[0:16, :] = p1
    w_ref[16:32, :] = p2
    w_ref[32:48, :] = p3


def target_rows(x, reg_sq):
    n = x[0] * x[0] + x[1] * x[1] + x[2] * x[2]
    one = jnp.ones_like(n)
    z = jnp.zeros_like(n)
    t = jnp.concatenate([-2.0 * x[0], -2.0 * x[1], -2.0 * x[2], one, n + reg_sq, z, z, z], axis=0)
    t1, t2, t3 = split3f(t)
    return jnp.concatenate([t1, t1, t1, t2, t2, t3], axis=0).astype(BF16), n


def weights(ya_ref, xa, hi_ref, lo_ref):
    d = lax.dot_general(ya_ref[...], xa, (((0,), (0,)), ((), ())), preferred_element_type=F32)
    s = lax.rsqrt(d)
    b = s * (s * s)
    hi = b.astype(BF16)
    hi_ref[...] = hi
    lo_ref[...] = (b - hi.astype(F32)).astype(BF16)


def contract(w_ref, hi_ref, lo_ref):
    p = jnp.dot(w_ref[...], hi_ref[...], preferred_element_type=F32)
    q = jnp.dot(w_ref[0:32, :], lo_ref[...], preferred_element_type=F32)
    return p[:16] + p[16:32] + p[32:] + q[:16] + q[16:]


def combine(acc, x, n, reg_sq):
    f = [acc[3:4], acc[7:8], acc[11:12]]
    yf = [[acc[4 * b + a : 4 * b + a + 1] for a in range(3)] for b in range(3)]
    z = [acc[12 + a : 13 + a] for a in range(3)]
    xf = x[0] * f[0] + x[1] * f[1] + x[2] * f[2] - (yf[0][0] + yf[1][1] + yf[2][2])
    out = []
    for a in range(3):
        t = (2 * reg_sq + n) * f[a] + z[a]
        for b in range(3):
            t = t - x[b] * (2.0 * yf[b][a] + yf[a][b])
        out.append(t + x[a] * xf)
    return out


def main_kernel(
    own_ref, tiles_ref, wide_ref, out_ref,
    big, coarse, xa_ref, acc_ref, ya0, ya1, w0, w1, hi0, hi1, lo0, lo1,
    near_send, near_recv, far_send, far_recv,
):
    blk = lax.axis_index("blk")
    nbr = lax.axis_index("nbr")
    zh = blk // YN
    y = lax.rem(blk, YN)

    def column(dz, dy):
        return (lax.rem(zh + dz, ZN) * YN + lax.rem(y + dy, YN), nbr)

    def row_peer(o):
        return (blk, lax.rem(nbr + o, PEERS))

    def far_copy(src, dz, dy, hop_z, hop_y):
        f = dz * YN + dy
        return pltpu.make_async_remote_copy(
            src_ref=src, dst_ref=big.at[FAR0 + f], send_sem=far_send.at[f], recv_sem=far_recv.at[f],
            device_id=column(hop_z, hop_y), device_id_type=MESH,
        )

    def near_copy(o):
        return pltpu.make_async_remote_copy(
            src_ref=tiles_ref.at[lax.rem(nbr + o, PEERS)], dst_ref=coarse.at[o - 1],
            send_sem=near_send.at[o - 1], recv_sem=near_recv.at[o - 1],
            device_id=row_peer(o), device_id_type=MESH,
        )

    barrier = pltpu.get_barrier_semaphore()
    for dz in (1, ZN - 1):
        pl.semaphore_signal(barrier, inc=1, device_id=column(dz, 0), device_id_type=MESH)

    def greet_row(o, c):
        pl.semaphore_signal(barrier, inc=1, device_id=row_peer(o), device_id_type=MESH)
        return c

    def greet_column(o, c):
        pl.semaphore_signal(barrier, inc=1, device_id=column(0, o), device_id_type=MESH)
        return c

    lax.fori_loop(1, YN, greet_column, 0)
    lax.fori_loop(1, PEERS, greet_row, 0)

    own = own_ref[...]
    big[FAR0] = own
    zero = jnp.zeros((1, 1), F32)
    means = [jnp.mean(own[i : i + 1], axis=1, keepdims=True) for i in range(3)]
    center = jnp.concatenate(means + [zero] * 5, axis=0)
    x = [own[i : i + 1] - means[i] for i in range(3)]
    xa_ref[0], n = target_rows(x, NEAR_REG_SQ)
    xa_ref[1], _ = target_rows(x, FAR_REG_SQ)
    acc_ref[...] = jnp.zeros_like(acc_ref)
    row = lax.broadcasted_iota(jnp.int32, (8, PTS), 0)
    u1, u2, u3 = split3(wide_ref[...])

    pl.semaphore_wait(barrier, 2 + (YN - 1) + (PEERS - 1))
    far_copy(own_ref, 1, 0, 1, 0).start()
    far_copy(own_ref, 3, 0, 3, 0).start()

    def send_near(o, c):
        near_copy(o).start()
        return c

    def send_own(o, c):
        far_copy(own_ref, 0, o, 0, o).start()
        return c

    def fan(dz):
        def send(o, c):
            far_copy(big.at[FAR0 + dz * YN], dz, o, 0, o).start()
            return c

        return send

    lax.fori_loop(1, PEERS, send_near, 0)
    lax.fori_loop(1, YN, send_own, 0)

    def take_near(o, c):
        near_copy(o).wait_recv()
        return c

    lax.fori_loop(1, PEERS, take_near, 0)
    far_copy(own_ref, 1, 0, 1, 0).wait_recv()
    far_copy(big.at[FAR0 + YN], 2, 0, 1, 0).start()
    lax.fori_loop(1, YN, fan(1), 0)
    far_copy(own_ref, 3, 0, 3, 0).wait_recv()
    lax.fori_loop(1, YN, fan(3), 0)

    a1, a2, a3 = split3(coarse[...].reshape(NEAR_BLOCKS * 8, 128))
    dot = functools.partial(jnp.dot, preferred_element_type=F32)
    fine = dot(a1, u1) + (dot(a1, u2) + dot(a2, u1)) + (dot(a1, u3) + dot(a2, u2) + dot(a3, u1))
    big[0:NEAR_BLOCKS] = fine.reshape(NEAR_BLOCKS, 8, PTS)

    ya = (ya0, ya1)
    w = (w0, w1)
    hi = (hi0, hi1)
    lo = (lo0, lo1)

    def kind(i):
        return jnp.where(i < FAR0, 0, 1)

    def step(i, p, first=False, last=False):
        q = 1 - p
        if not first:
            s = kind(i - 1)
            acc_ref[s] += contract(w[q], hi[q], lo[q])
        weights(ya[p], xa_ref[kind(i)], hi[p], lo[p])
        if not last:
            prepare(big[i + 1], center, row, ya[q], w[q])

    def take_far(f):
        @pl.when(lax.rem(f, YN) != 0)
        def _():
            far_copy(own_ref, 0, f, 0, 1).wait_recv()

    def pair(k, c):
        step(2 * k + 1, 1)
        step(2 * k + 2, 0)
        return c

    def far_pair(k, c):
        take_far(2 * k + 2 - FAR0)
        take_far(2 * k + 3 - FAR0)
        return pair(k, c)

    prepare(big[0], center, row, ya0, w0)
    step(0, 0, first=True)
    lax.fori_loop(0, 4, pair, 0)
    far_copy(big.at[FAR0 + YN], 2, 0, 1, 0).wait_recv()
    lax.fori_loop(1, YN, fan(2), 0)
    lax.fori_loop(4, 15, pair, 0)
    lax.fori_loop(15, 30, far_pair, 0)
    take_far(BLOCKS - 1 - FAR0)
    step(BLOCKS - 2, 1)
    step(BLOCKS - 1, 0, last=True)
    acc_ref[1] += contract(w0, hi0, lo0)

    near = combine(acc_ref[0], x, n, NEAR_REG_SQ)
    far = combine(acc_ref[1], x, n, FAR_REG_SQ)
    for a in range(3):
        out_ref[a : a + 1, :] = STOKES_COEF * (far[a] + near[a])

    def sent_near(o, c):
        near_copy(o).wait_send()
        return c

    def sent_far(f, c):
        far_copy(own_ref, 0, f, 0, 1).wait_send()
        return c

    lax.fori_loop(1, PEERS, sent_near, 0)
    lax.fori_loop(1, ZN * YN, sent_far, 0)


def shards(positions, density, upsample, cell_map, near_list):
    vmem = pl.BlockSpec(memory_space=pltpu.VMEM)
    smem = pl.BlockSpec(memory_space=pltpu.SMEM)
    own, tiles, wide = pl.pallas_call(
        pack_kernel,
        out_shape=(
            jax.ShapeDtypeStruct((8, PTS), F32),
            jax.ShapeDtypeStruct((PEERS + 1, 8, 128), F32),
            jax.ShapeDtypeStruct((128, PTS), F32),
        ),
        in_specs=[smem, smem, vmem, vmem, vmem],
        out_specs=(vmem, vmem, vmem),
        scratch_shapes=[pltpu.VMEM((16, 8, 128), F32), pltpu.SMEM((PEERS + 1,), jnp.int32)],
    )(near_list.reshape(-1), cell_map, positions, density, upsample)
    return pl.pallas_call(
        main_kernel,
        out_shape=jax.ShapeDtypeStruct((3, PTS), F32),
        in_specs=[vmem, vmem, vmem],
        out_specs=vmem,
        scratch_shapes=[
            pltpu.VMEM((BLOCKS, 8, PTS), F32),
            pltpu.VMEM((NEAR_BLOCKS, 8, 128), F32),
            pltpu.VMEM((2, 48, PTS), BF16),
            pltpu.VMEM((2, 16, PTS), F32),
        ]
        + [pltpu.VMEM((48, PTS), BF16)] * 4
        + [pltpu.VMEM((PTS, PTS), BF16)] * 4
        + [pltpu.SemaphoreType.DMA((NEAR_BLOCKS,))] * 2
        + [pltpu.SemaphoreType.DMA((ZN * YN,))] * 2,
        compiler_params=pltpu.CompilerParams(
            collective_id=0, has_side_effects=True, vmem_limit_bytes=48 << 20
        ),
    )(own, tiles, wide)


def solution(mesh):
    placed = (
        P(None, ("blk", "nbr")),
        P(None, ("blk", "nbr")),
        P(),
        P("blk", None),
        P(("blk", "nbr"), None, None),
    )
    return jax.shard_map(
        shards, mesh=mesh, in_specs=placed, out_specs=P(None, ("blk", "nbr")), check_vma=False
    )
```

```python
import functools
import math

import jax
import jax.numpy as jnp
from jax import lax
from jax.experimental import pallas as pl
from jax.experimental.pallas import tpu as pltpu
from jax.sharding import PartitionSpec as P

F32 = jnp.float32
BF16 = jnp.bfloat16
MESH = pl.DeviceIdType.MESH
FAR_REG_SQ = 0.0625
NEAR_REG_SQ = 0.01
STOKES_COEF = 1.0 / (8.0 * math.pi)

PTS = 512
PANELS = 16
SLOTS = 4
PEERS = 32
ZN = 4
YN = 8
XN = 4
NEAR_FIRST = 8
COLUMN = ZN * YN
FAR0 = PEERS - 1
BLOCKS = FAR0 + COLUMN
CHUNK = 64


def split3(a):
    a1 = a.astype(BF16)
    r = a - a1.astype(F32)
    a2 = r.astype(BF16)
    r = r - a2.astype(F32)
    return a1, a2, r.astype(BF16)


def split3f(a):
    a1 = a.astype(BF16).astype(F32)
    r = a - a1
    a2 = r.astype(BF16).astype(F32)
    return a1, a2, r - a2


def bc(t, r):
    return jnp.broadcast_to(t[r : r + 1, :], t.shape)


def prepare(t, center, row, ya_ref, w_ref):
    tc = t - center
    g = pltpu.roll(tc, 4, 0)
    sq = tc * tc
    df = tc * g
    nb = jnp.broadcast_to(sq[0:1] + sq[1:2] + sq[2:3], t.shape)
    db = jnp.broadcast_to(df[0:1] + df[1:2] + df[2:3], t.shape)
    s = jnp.where(row < 3, tc, jnp.where(row == 3, nb, jnp.where(row == 4, 1.0, 0.0)))
    s1, s2, s3 = split3f(s)
    ya_ref[...] = jnp.concatenate([s1, s2, s3, s1, s2, s1], axis=0).astype(BF16)
    low = row < 4
    f2 = jnp.where(low, g, tc)
    w1 = jnp.where(low, bc(tc, 0), bc(tc, 1)) * f2
    w2 = jnp.where(low, bc(tc, 2) * g, nb * tc + db * g)
    w1 = jnp.where(row == 3, bc(tc, 4), jnp.where(row == 7, bc(tc, 5), w1))
    w2 = jnp.where(row == 3, bc(tc, 6), w2)
    p1, p2, p3 = split3(jnp.concatenate([w1, w2], axis=0))
    for o in (0, PTS):
        w_ref[0:16, o : o + PTS] = p1
        w_ref[16:32, o : o + PTS] = p2
        w_ref[32:48, o : o + PTS] = p3


def target_rows(x, reg_sq):
    n = x[0] * x[0] + x[1] * x[1] + x[2] * x[2]
    one = jnp.ones_like(n)
    z = jnp.zeros_like(n)
    t = jnp.concatenate([-2.0 * x[0], -2.0 * x[1], -2.0 * x[2], one, n + reg_sq, z, z, z], axis=0)
    t1, t2, t3 = split3f(t)
    return jnp.concatenate([t1, t1, t1, t2, t2, t3], axis=0).astype(BF16), n


def distances(ya_ref, r, n, xa, d_ref):
    d_ref[r : r + n, :] = lax.dot_general(
        ya_ref[:, r : r + n], xa, (((0,), (0,)), ((), ())), preferred_element_type=F32
    )


def weights(d_ref, r, n, b_ref):
    s = lax.rsqrt(d_ref[r : r + n, :])
    b = s * (s * s)
    hi = b.astype(BF16)
    b_ref[r : r + n, :] = hi
    b_ref[PTS + r : PTS + r + n, :] = (b - hi.astype(F32)).astype(BF16)


def contract(w_ref, b_ref):
    p = jnp.dot(w_ref[...], b_ref[...], preferred_element_type=F32)
    return p[:16] + p[16:32] + p[32:]


def combine(acc, x, n, reg_sq):
    f = [acc[3:4], acc[7:8], acc[11:12]]
    yf = [[acc[4 * b + a : 4 * b + a + 1] for a in range(3)] for b in range(3)]
    z = [acc[12 + a : 13 + a] for a in range(3)]
    xf = x[0] * f[0] + x[1] * f[1] + x[2] * f[2] - (yf[0][0] + yf[1][1] + yf[2][2])
    out = []
    for a in range(3):
        t = (2 * reg_sq + n) * f[a] + z[a]
        for b in range(3):
            t = t - x[b] * (2.0 * yf[b][a] + yf[a][b])
        out.append(t + x[a] * xf)
    return out


def upsampled(tiles, up):
    a1, a2, a3 = split3(tiles.reshape(-1, 128))
    u1, u2, u3 = up
    dot = functools.partial(jnp.dot, preferred_element_type=F32)
    fine = dot(a1, u1) + (dot(a1, u2) + dot(a2, u1)) + (dot(a1, u3) + dot(a2, u2) + dot(a3, u1))
    return fine.reshape(-1, 8, PTS)


def main_kernel(
    pos_hbm, den_hbm, up_hbm, map_hbm, list_hbm, out_ref,
    pos_ref, den_ref, up_ref, map_ref, list_ref, ids_ref, ids_smem, table, tiles, wide,
    own_ref, coarse, big, xa_ref, acc_ref, ya0, ya1, w0, w1, w2, w3, d0, d1, b0, b1,
    load_sem, near_send, near_recv, far_send, far_recv,
):
    blk = lax.axis_index("blk")
    nbr = lax.axis_index("nbr")
    zh = blk // YN
    y = lax.rem(blk, YN)
    zl = nbr // (2 * XN)
    xc = lax.rem(nbr // 2, XN)
    core = lax.rem(nbr, 2)

    def column(dz, dy):
        return (lax.rem(zh + dz, ZN) * YN + lax.rem(y + dy, YN), nbr)

    def row_index(o):
        dz = o // (2 * XN)
        dx = lax.rem(o // 2, XN)
        dc = lax.rem(o, 2)
        return (lax.rem(zl + dz, ZN) * XN + lax.rem(xc + dx, XN)) * 2 + lax.rem(core + dc, 2)

    def far_copy(src, dz, dy, hop_z, hop_y):
        f = dz * YN + dy
        return pltpu.make_async_remote_copy(
            src_ref=src, dst_ref=big.at[FAR0 + f], send_sem=far_send.at[f], recv_sem=far_recv.at[f],
            device_id=column(hop_z, hop_y), device_id_type=MESH,
        )

    def near_copy(o):
        return pltpu.make_async_remote_copy(
            src_ref=tiles.at[o], dst_ref=coarse.at[o - 1],
            send_sem=near_send.at[o - 1], recv_sem=near_recv.at[o - 1],
            device_id=(blk, row_index(o)), device_id_type=MESH,
        )

    loads = [
        pltpu.make_async_copy(src, dst, load_sem.at[q])
        for q, (src, dst) in enumerate(
            ((list_hbm, list_ref), (map_hbm, map_ref), (pos_hbm, pos_ref), (den_hbm, den_ref), (up_hbm, up_ref))
        )
    ]
    for load in loads:
        load.start()
    barrier = pltpu.get_barrier_semaphore()
    for dz in (1, ZN - 1):
        pl.semaphore_signal(barrier, inc=1, device_id=column(dz, 0), device_id_type=MESH)

    def greet_row(o, c):
        pl.semaphore_signal(barrier, inc=1, device_id=(blk, row_index(PEERS - o)), device_id_type=MESH)
        return c

    def greet_column(o, c):
        pl.semaphore_signal(barrier, inc=1, device_id=column(0, o), device_id_type=MESH)
        return c

    lax.fori_loop(1, PEERS, greet_row, 0)
    lax.fori_loop(1, YN, greet_column, 0)
    for load in loads:
        load.wait()

    peer_row = lax.broadcasted_iota(jnp.int32, (PEERS, PEERS), 0)
    place = jnp.where(peer_row == map_ref[...], 1.0, 0.0).astype(BF16)
    entries = list_ref.shape[1]
    ids = list_ref[...]
    panel = ids[0:1, :]
    target = ids[1:2, :]
    cell = lax.broadcasted_iota(jnp.int32, (PEERS, entries), 0)
    named = jnp.where(cell == target, 1.0, 0.0).astype(BF16)
    hit = jnp.dot(place, named, preferred_element_type=F32)
    before = jnp.where(
        lax.broadcasted_iota(jnp.int32, (entries, entries), 0) < lax.broadcasted_iota(jnp.int32, (entries, entries), 1),
        1.0, 0.0,
    ).astype(BF16)
    rank = jnp.dot(hit.astype(BF16), before, preferred_element_type=F32)
    number = (panel + 1).astype(F32)
    lane = lax.broadcasted_iota(jnp.int32, (PEERS, 128), 1)
    chosen = jnp.zeros((PEERS, 128), F32)
    for s in range(SLOTS):
        value = jnp.sum(jnp.where((hit > 0.5) & (rank == s), number, 0.0), axis=1, keepdims=True)
        chosen = jnp.where(lane == s, value, chosen)
    ids_ref[...] = chosen.astype(jnp.int32)
    to_smem = pltpu.make_async_copy(ids_ref, ids_smem, load_sem.at[0])
    to_smem.start()

    zero = jnp.zeros((1, PTS), F32)
    own = jnp.concatenate([pos_ref[...], zero, den_ref[...], zero], axis=0)
    own_ref[...] = own
    big[FAR0] = own
    upper = lax.broadcasted_iota(jnp.int32, (8, 128), 0) < 4
    for v in range(4):
        part = own[:, 128 * v : 128 * v + 128]
        part = jnp.where(upper, part, 0.25 * part)
        for r in range(4):
            table[4 * v + r] = part if r == 0 else pltpu.roll(part, 32 * r, 1)
    table[PANELS] = jnp.zeros((8, 128), F32)
    lane_slot = lax.broadcasted_iota(jnp.int32, (8, 128), 1) // 32
    to_smem.wait()

    def route(o, c):
        peer = row_index(o)
        tile = jnp.zeros((8, 128), F32)
        for s in range(SLOTS):
            k = jnp.minimum(jnp.maximum(ids_smem[peer, s] - 1, -1), PANELS - 1)
            at = jnp.where(k < 0, PANELS, 4 * (k // 4) + jnp.bitwise_and(s - k, 3))
            at = jnp.minimum(jnp.maximum(at, 0), PANELS)
            tile = jnp.where(lane_slot == s, table[at], tile)
        tiles[o] = tile
        return c

    lax.fori_loop(1, PEERS, route, 0)

    up = up_ref[...]
    none = jnp.zeros_like(up)
    for s in range(SLOTS):
        wide[32 * s : 32 * s + 32, :] = jnp.concatenate([up if q == s else none for q in range(SLOTS)], axis=1)
    z1 = jnp.zeros((1, 1), F32)
    means = [jnp.mean(own[i : i + 1], axis=1, keepdims=True) for i in range(3)]
    center = jnp.concatenate(means + [z1] * 5, axis=0)
    x = [own[i : i + 1] - means[i] for i in range(3)]
    xa_ref[0], n = target_rows(x, NEAR_REG_SQ)
    xa_ref[1], _ = target_rows(x, FAR_REG_SQ)
    acc_ref[...] = jnp.zeros_like(acc_ref)
    b1[...] = jnp.zeros_like(b1)
    w3[...] = jnp.zeros_like(w3)
    row = lax.broadcasted_iota(jnp.int32, (8, PTS), 0)

    pl.semaphore_wait(barrier, 2 + (YN - 1) + (PEERS - 1))
    far_copy(own_ref, 1, 0, 1, 0).start()
    far_copy(own_ref, 3, 0, 3, 0).start()

    def send_near(o, c):
        near_copy(o).start()
        return c

    def send_own(o, c):
        far_copy(own_ref, 0, o, 0, o).start()
        return c

    def take_near(o, c):
        near_copy(o).wait_recv()
        return c

    def fan(dz):
        def send(o, c):
            far_copy(big.at[FAR0 + dz * YN], dz, o, 0, o).start()
            return c

        return send

    lax.fori_loop(1, PEERS, send_near, 0)
    lax.fori_loop(1, YN, send_own, 0)

    ya = (ya0, ya1)
    w = (w0, w1, w2, w3)
    d = (d0, d1)
    b = (b0, b1)

    def block(i):
        return jnp.where(i == 0, FAR0, jnp.where(i < PEERS, i - 1, i))

    def kind(i):
        return jnp.where(i == 0, 1, jnp.where(i < PEERS, 0, 1))

    def prep(i, j):
        prepare(big[block(i)], center, row, ya[j % 2], w[j % 4])

    def step(i, j, more=2):
        p = j % 2
        q = 1 - p
        half = PTS // 2
        xa = xa_ref[kind(i + 1)]
        if more > 0:
            distances(ya[q], 0, half, xa, d[q])
        acc_ref[kind(i - 1)] += contract(w[(j - 1) % 4], b[q])
        for r in range(4):
            weights(d[p], CHUNK * r, CHUNK, b[p])
        if more > 0:
            distances(ya[q], half, half, xa, d[q])
        for r in range(4, 8):
            weights(d[p], CHUNK * r, CHUNK, b[p])
        if more > 1:
            prep(i + 2, j + 2)

    prep(0, 0)
    distances(ya0, 0, PTS, xa_ref[1], d0)
    lax.fori_loop(1, NEAR_FIRST, take_near, 0)
    fine = functools.partial(upsampled, up=split3(wide[...]))
    big[0 : NEAR_FIRST - 1] = fine(coarse[0 : NEAR_FIRST - 1])
    prep(1, 1)

    def take_far(f):
        @pl.when((f > 0) & (lax.rem(f, YN) != 0))
        def _():
            far_copy(own_ref, 0, f, 0, 1).wait_recv()

    def body(k, c):
        @pl.when(k == 1)
        def _():
            far_copy(own_ref, 1, 0, 1, 0).wait_recv()
            far_copy(big.at[FAR0 + YN], 2, 0, 1, 0).start()
            lax.fori_loop(1, YN, fan(1), 0)
            far_copy(own_ref, 3, 0, 3, 0).wait_recv()
            lax.fori_loop(1, YN, fan(3), 0)
            lax.fori_loop(NEAR_FIRST, PEERS, take_near, 0)
            big[NEAR_FIRST - 1 : FAR0] = fine(coarse[NEAR_FIRST - 1 : FAR0])

        @pl.when(k == 3)
        def _():
            far_copy(big.at[FAR0 + YN], 2, 0, 1, 0).wait_recv()
            lax.fori_loop(1, YN, fan(2), 0)

        for j in range(4):
            take_far(4 * k + j + 2 - FAR0)
        for j in range(4):
            step(4 * k + j, j)
        return c

    lax.fori_loop(0, 15, body, 0)
    take_far(BLOCKS - 1 - FAR0)
    step(BLOCKS - 3, 0)
    step(BLOCKS - 2, 1, more=1)
    step(BLOCKS - 1, 2, more=0)
    acc_ref[1] += contract(w2, b0)

    near = combine(acc_ref[0], x, n, NEAR_REG_SQ)
    far = combine(acc_ref[1], x, n, FAR_REG_SQ)
    for a in range(3):
        out_ref[a : a + 1, :] = STOKES_COEF * (far[a] + near[a])

    def sent_near(o, c):
        near_copy(o).wait_send()
        return c

    def sent_far(f, c):
        far_copy(own_ref, 0, f, 0, 1).wait_send()
        return c

    lax.fori_loop(1, PEERS, sent_near, 0)
    lax.fori_loop(1, COLUMN, sent_far, 0)


def shards(positions, density, upsample, cell_map, near_list):
    entries = near_list.shape[1]
    anywhere = pl.BlockSpec(memory_space=pl.ANY)
    return pl.pallas_call(
        main_kernel,
        out_shape=jax.ShapeDtypeStruct((3, PTS), F32),
        in_specs=[anywhere] * 5,
        out_specs=pl.BlockSpec(memory_space=pltpu.VMEM),
        scratch_shapes=[
            pltpu.VMEM((3, PTS), F32),
            pltpu.VMEM((3, PTS), F32),
            pltpu.VMEM(upsample.shape, F32),
            pltpu.VMEM((1, PEERS), jnp.int32),
            pltpu.VMEM((2, entries), jnp.int32),
            pltpu.VMEM((PEERS, 128), jnp.int32),
            pltpu.SMEM((PEERS, 128), jnp.int32),
            pltpu.VMEM((PANELS + 1, 8, 128), F32),
            pltpu.VMEM((PEERS, 8, 128), F32),
            pltpu.VMEM((128, PTS), F32),
            pltpu.VMEM((8, PTS), F32),
            pltpu.VMEM((PEERS - 1, 8, 128), F32),
            pltpu.VMEM((BLOCKS, 8, PTS), F32),
            pltpu.VMEM((2, 48, PTS), BF16),
            pltpu.VMEM((2, 16, PTS), F32),
        ]
        + [pltpu.VMEM((48, PTS), BF16)] * 2
        + [pltpu.VMEM((48, 2 * PTS), BF16)] * 4
        + [pltpu.VMEM((PTS, PTS), F32)] * 2
        + [pltpu.VMEM((2 * PTS, PTS), BF16)] * 2
        + [pltpu.SemaphoreType.DMA((5,))]
        + [pltpu.SemaphoreType.DMA((PEERS - 1,))] * 2
        + [pltpu.SemaphoreType.DMA((COLUMN,))] * 2,
        compiler_params=pltpu.CompilerParams(
            collective_id=0, has_side_effects=True, vmem_limit_bytes=62 << 20
        ),
    )(positions, density, upsample, cell_map, jnp.transpose(near_list, (0, 2, 1)).reshape(2, entries))


def solution(mesh):
    placed = (
        P(None, ("blk", "nbr")),
        P(None, ("blk", "nbr")),
        P(),
        P("blk", None),
        P(("blk", "nbr"), None, None),
    )
    return jax.shard_map(
        shards, mesh=mesh, in_specs=placed, out_specs=P(None, ("blk", "nbr")), check_vma=False
    )
```

```python
import functools
import math

import jax
import jax.numpy as jnp
from jax import lax
from jax.experimental import pallas as pl
from jax.experimental.pallas import tpu as pltpu
from jax.sharding import PartitionSpec as P

F32 = jnp.float32
BF16 = jnp.bfloat16
MESH = pl.DeviceIdType.MESH
FAR_REG_SQ = 0.0625
NEAR_REG_SQ = 0.01
STOKES_COEF = 1.0 / (8.0 * math.pi)

PTS = 512
PANELS = 16
SLOTS = 4
PEERS = 32
ZN = 4
YN = 8
XN = 4
NEAR_FIRST = 8
COLUMN = ZN * YN
FAR0 = PEERS - 1
BLOCKS = FAR0 + COLUMN
CHUNK = 64


def split3(a):
    a1 = a.astype(BF16)
    r = a - a1.astype(F32)
    a2 = r.astype(BF16)
    r = r - a2.astype(F32)
    return a1, a2, r.astype(BF16)


def split3f(a):
    a1 = a.astype(BF16).astype(F32)
    r = a - a1
    a2 = r.astype(BF16).astype(F32)
    return a1, a2, r - a2


def bc(t, r):
    return jnp.broadcast_to(t[r : r + 1, :], t.shape)


def prepare(t, center, row, ya_ref, w_ref):
    tc = t - center
    g = pltpu.roll(tc, 4, 0)
    sq = tc * tc
    df = tc * g
    nb = jnp.broadcast_to(sq[0:1] + sq[1:2] + sq[2:3], t.shape)
    db = jnp.broadcast_to(df[0:1] + df[1:2] + df[2:3], t.shape)
    s = jnp.where(row < 3, tc, jnp.where(row == 3, nb, jnp.where(row == 4, 1.0, 0.0)))
    s1, s2, s3 = split3f(s)
    ya_ref[...] = jnp.concatenate([s1, s2, s3, s1, s2, s1], axis=0).astype(BF16)
    low = row < 4
    f2 = jnp.where(low, g, tc)
    w1 = jnp.where(low, bc(tc, 0), bc(tc, 1)) * f2
    w2 = jnp.where(low, bc(tc, 2) * g, nb * tc + db * g)
    w1 = jnp.where(row == 3, bc(tc, 4), jnp.where(row == 7, bc(tc, 5), w1))
    w2 = jnp.where(row == 3, bc(tc, 6), w2)
    p1, p2, p3 = split3(jnp.concatenate([w1, w2], axis=0))
    w_ref[0:16, :] = p1
    w_ref[16:32, :] = p2
    w_ref[32:48, :] = p3


def target_rows(x, reg_sq):
    n = x[0] * x[0] + x[1] * x[1] + x[2] * x[2]
    one = jnp.ones_like(n)
    z = jnp.zeros_like(n)
    t = jnp.concatenate([-2.0 * x[0], -2.0 * x[1], -2.0 * x[2], one, n + reg_sq, z, z, z], axis=0)
    t1, t2, t3 = split3f(t)
    return jnp.concatenate([t1, t1, t1, t2, t2, t3], axis=0).astype(BF16), n


def distances(ya_ref, r, n, xa, d_ref):
    d_ref[r : r + n, :] = lax.dot_general(
        ya_ref[:, r : r + n], xa, (((0,), (0,)), ((), ())), preferred_element_type=F32
    )


def weights(d_ref, r, n, b_ref):
    s = lax.rsqrt(d_ref[r : r + n, :])
    b = s * (s * s)
    hi = b.astype(BF16)
    b_ref[r : r + n, :] = hi
    b_ref[PTS + r : PTS + r + n, :] = (b - hi.astype(F32)).astype(BF16)


def contract_hi(w_ref, b_ref):
    p = jnp.dot(w_ref[...], b_ref[0:PTS, :], preferred_element_type=F32)
    return p[:16] + p[16:32] + p[32:]


def contract_lo(w_ref, b_ref):
    p = jnp.dot(w_ref[0:32, :], b_ref[PTS : 2 * PTS, :], preferred_element_type=F32)
    return p[:16] + p[16:]


def combine(acc, x, n, reg_sq):
    f = [acc[3:4], acc[7:8], acc[11:12]]
    yf = [[acc[4 * b + a : 4 * b + a + 1] for a in range(3)] for b in range(3)]
    z = [acc[12 + a : 13 + a] for a in range(3)]
    xf = x[0] * f[0] + x[1] * f[1] + x[2] * f[2] - (yf[0][0] + yf[1][1] + yf[2][2])
    out = []
    for a in range(3):
        t = (2 * reg_sq + n) * f[a] + z[a]
        for b in range(3):
            t = t - x[b] * (2.0 * yf[b][a] + yf[a][b])
        out.append(t + x[a] * xf)
    return out


def upsampled(tiles, up):
    a1, a2, a3 = split3(tiles.reshape(-1, 128))
    u1, u2, u3 = up
    dot = functools.partial(jnp.dot, preferred_element_type=F32)
    fine = dot(a1, u1) + (dot(a1, u2) + dot(a2, u1)) + (dot(a1, u3) + dot(a2, u2) + dot(a3, u1))
    return fine.reshape(-1, 8, PTS)


def main_kernel(
    pos_hbm, den_hbm, up_hbm, map_hbm, list_hbm, out_ref,
    pos_ref, den_ref, up_ref, map_ref, list_ref, ids_ref, ids_smem, table, tiles, wide,
    own_ref, coarse, big, xa_ref, acc_ref, ya0, ya1, w0, w1, w2, w3, d0, d1, b0, b1,
    load_sem, near_send, near_recv, far_send, far_recv,
):
    blk = lax.axis_index("blk")
    nbr = lax.axis_index("nbr")
    zh = blk // YN
    y = lax.rem(blk, YN)
    zl = nbr // (2 * XN)
    xc = lax.rem(nbr // 2, XN)
    core = lax.rem(nbr, 2)

    def column(dz, dy):
        return (lax.rem(zh + dz, ZN) * YN + lax.rem(y + dy, YN), nbr)

    def row_index(o):
        dz = o // (2 * XN)
        dx = lax.rem(o // 2, XN)
        dc = lax.rem(o, 2)
        return (lax.rem(zl + dz, ZN) * XN + lax.rem(xc + dx, XN)) * 2 + lax.rem(core + dc, 2)

    def far_copy(src, dz, dy, hop_z, hop_y):
        f = dz * YN + dy
        return pltpu.make_async_remote_copy(
            src_ref=src, dst_ref=big.at[FAR0 + f], send_sem=far_send.at[f], recv_sem=far_recv.at[f],
            device_id=column(hop_z, hop_y), device_id_type=MESH,
        )

    def near_copy(o):
        return pltpu.make_async_remote_copy(
            src_ref=tiles.at[o], dst_ref=coarse.at[o - 1],
            send_sem=near_send.at[o - 1], recv_sem=near_recv.at[o - 1],
            device_id=(blk, row_index(o)), device_id_type=MESH,
        )

    loads = [
        pltpu.make_async_copy(src, dst, load_sem.at[q])
        for q, (src, dst) in enumerate(
            ((list_hbm, list_ref), (map_hbm, map_ref), (pos_hbm, pos_ref), (den_hbm, den_ref), (up_hbm, up_ref))
        )
    ]
    for load in loads:
        load.start()
    barrier = pltpu.get_barrier_semaphore()
    for dz in (1, ZN - 1):
        pl.semaphore_signal(barrier, inc=1, device_id=column(dz, 0), device_id_type=MESH)

    def greet_row(o, c):
        pl.semaphore_signal(barrier, inc=1, device_id=(blk, row_index(PEERS - o)), device_id_type=MESH)
        return c

    def greet_column(o, c):
        pl.semaphore_signal(barrier, inc=1, device_id=column(0, o), device_id_type=MESH)
        return c

    lax.fori_loop(1, PEERS, greet_row, 0)
    lax.fori_loop(1, YN, greet_column, 0)
    for load in loads:
        load.wait()

    peer_row = lax.broadcasted_iota(jnp.int32, (PEERS, PEERS), 0)
    place = jnp.where(peer_row == map_ref[...], 1.0, 0.0).astype(BF16)
    entries = list_ref.shape[1]
    ids = list_ref[...]
    panel = ids[0:1, :]
    target = ids[1:2, :]
    cell = lax.broadcasted_iota(jnp.int32, (PEERS, entries), 0)
    named = jnp.where(cell == target, 1.0, 0.0).astype(BF16)
    hit = jnp.dot(place, named, preferred_element_type=F32)
    before = jnp.where(
        lax.broadcasted_iota(jnp.int32, (entries, entries), 0) < lax.broadcasted_iota(jnp.int32, (entries, entries), 1),
        1.0, 0.0,
    ).astype(BF16)
    rank = jnp.dot(hit.astype(BF16), before, preferred_element_type=F32)
    number = (panel + 1).astype(F32)
    lane = lax.broadcasted_iota(jnp.int32, (PEERS, 128), 1)
    chosen = jnp.zeros((PEERS, 128), F32)
    for s in range(SLOTS):
        value = jnp.sum(jnp.where((hit > 0.5) & (rank == s), number, 0.0), axis=1, keepdims=True)
        chosen = jnp.where(lane == s, value, chosen)
    ids_ref[...] = chosen.astype(jnp.int32)
    to_smem = pltpu.make_async_copy(ids_ref, ids_smem, load_sem.at[0])
    to_smem.start()

    zero = jnp.zeros((1, PTS), F32)
    own = jnp.concatenate([pos_ref[...], zero, den_ref[...], zero], axis=0)
    own_ref[...] = own
    big[FAR0] = own
    upper = lax.broadcasted_iota(jnp.int32, (8, 128), 0) < 4
    for v in range(4):
        part = own[:, 128 * v : 128 * v + 128]
        part = jnp.where(upper, part, 0.25 * part)
        for r in range(4):
            table[4 * v + r] = part if r == 0 else pltpu.roll(part, 32 * r, 1)
    table[PANELS] = jnp.zeros((8, 128), F32)
    lane_slot = lax.broadcasted_iota(jnp.int32, (8, 128), 1) // 32
    to_smem.wait()

    def route(o, c):
        peer = row_index(o)
        tile = jnp.zeros((8, 128), F32)
        for s in range(SLOTS):
            k = jnp.minimum(jnp.maximum(ids_smem[peer, s] - 1, -1), PANELS - 1)
            at = jnp.where(k < 0, PANELS, 4 * (k // 4) + jnp.bitwise_and(s - k, 3))
            at = jnp.minimum(jnp.maximum(at, 0), PANELS)
            tile = jnp.where(lane_slot == s, table[at], tile)
        tiles[o] = tile
        return c

    lax.fori_loop(1, PEERS, route, 0)

    up = up_ref[...]
    none = jnp.zeros_like(up)
    for s in range(SLOTS):
        wide[32 * s : 32 * s + 32, :] = jnp.concatenate([up if q == s else none for q in range(SLOTS)], axis=1)
    z1 = jnp.zeros((1, 1), F32)
    means = [jnp.mean(own[i : i + 1], axis=1, keepdims=True) for i in range(3)]
    center = jnp.concatenate(means + [z1] * 5, axis=0)
    x = [own[i : i + 1] - means[i] for i in range(3)]
    xa_ref[0], n = target_rows(x, NEAR_REG_SQ)
    xa_ref[1], _ = target_rows(x, FAR_REG_SQ)
    acc_ref[...] = jnp.zeros_like(acc_ref)
    b1[...] = jnp.zeros_like(b1)
    w3[...] = jnp.zeros_like(w3)
    row = lax.broadcasted_iota(jnp.int32, (8, PTS), 0)

    pl.semaphore_wait(barrier, 2 + (YN - 1) + (PEERS - 1))
    far_copy(own_ref, 1, 0, 1, 0).start()
    far_copy(own_ref, 3, 0, 3, 0).start()

    def send_near(o, c):
        near_copy(o).start()
        return c

    def send_own(o, c):
        far_copy(own_ref, 0, o, 0, o).start()
        return c

    def take_near(o, c):
        near_copy(o).wait_recv()
        return c

    def fan(dz):
        def send(o, c):
            far_copy(big.at[FAR0 + dz * YN], dz, o, 0, o).start()
            return c

        return send

    lax.fori_loop(1, PEERS, send_near, 0)
    lax.fori_loop(1, YN, send_own, 0)

    ya = (ya0, ya1)
    w = (w0, w1, w2, w3)
    d = (d0, d1)
    b = (b0, b1)

    def block(i):
        late = jnp.where(i < 47, i, jnp.where(i < 55, i + 8, i - 8))
        far = jnp.where(i == 0, FAR0, jnp.where(i < 15, FAR0 - 7 + i, late))
        return jnp.where(kind(i) == 1, far, jnp.where(i < 15, i - 1, i - 8))

    def kind(i):
        return jnp.where(i == 0, 1, jnp.where(i < 8, 0, jnp.where(i < 15, 1, jnp.where(i < 39, 0, 1))))

    def prep(i, j):
        prepare(big[block(i)], center, row, ya[j % 2], w[j % 4])

    def step(i, j, more=2):
        p = j % 2
        q = 1 - p
        half = PTS // 2
        xa = xa_ref[kind(i + 1)]
        before_kind = kind(i - 1)
        before_w = w[(j - 1) % 4]
        acc_ref[before_kind] += contract_hi(before_w, b[q])
        if more > 0:
            distances(ya[q], 0, half, xa, d[q])
        for r in range(4):
            weights(d[p], CHUNK * r, CHUNK, b[p])
        acc_ref[before_kind] += contract_lo(before_w, b[q])
        if more > 0:
            distances(ya[q], half, half, xa, d[q])
        for r in range(4, 8):
            weights(d[p], CHUNK * r, CHUNK, b[p])
        if more > 1:
            prep(i + 2, j + 2)

    prep(0, 0)
    distances(ya0, 0, PTS, xa_ref[1], d0)
    lax.fori_loop(1, NEAR_FIRST, take_near, 0)
    fine = functools.partial(upsampled, up=split3(wide[...]))
    big[0 : NEAR_FIRST - 1] = fine(coarse[0 : NEAR_FIRST - 1])
    prep(1, 1)

    def take_far(i):
        f = block(i) - FAR0

        @pl.when((kind(i) == 1) & (lax.rem(f, YN) != 0))
        def _():
            far_copy(own_ref, 0, f, 0, 1).wait_recv()

    def body(k, c):
        @pl.when(k == 2)
        def _():
            far_copy(own_ref, 1, 0, 1, 0).wait_recv()
            far_copy(big.at[FAR0 + YN], 2, 0, 1, 0).start()
            lax.fori_loop(1, YN, fan(1), 0)
            far_copy(own_ref, 3, 0, 3, 0).wait_recv()
            lax.fori_loop(1, YN, fan(3), 0)

        @pl.when(k == 3)
        def _():
            lax.fori_loop(NEAR_FIRST, PEERS, take_near, 0)
            big[NEAR_FIRST - 1 : FAR0] = fine(coarse[NEAR_FIRST - 1 : FAR0])

        @pl.when(k == 5)
        def _():
            far_copy(big.at[FAR0 + YN], 2, 0, 1, 0).wait_recv()
            lax.fori_loop(1, YN, fan(2), 0)

        for j in range(4):
            take_far(4 * k + j + 2)
        for j in range(4):
            step(4 * k + j, j)
        return c

    lax.fori_loop(0, 15, body, 0)
    take_far(BLOCKS - 1)
    step(BLOCKS - 3, 0)
    step(BLOCKS - 2, 1, more=1)
    step(BLOCKS - 1, 2, more=0)
    acc_ref[1] += contract_hi(w2, b0) + contract_lo(w2, b0)

    near = combine(acc_ref[0], x, n, NEAR_REG_SQ)
    far = combine(acc_ref[1], x, n, FAR_REG_SQ)
    for a in range(3):
        out_ref[a : a + 1, :] = STOKES_COEF * (far[a] + near[a])

    def sent_near(o, c):
        near_copy(o).wait_send()
        return c

    def sent_far(f, c):
        far_copy(own_ref, 0, f, 0, 1).wait_send()
        return c

    lax.fori_loop(1, PEERS, sent_near, 0)
    lax.fori_loop(1, COLUMN, sent_far, 0)


def shards(positions, density, upsample, cell_map, near_list):
    entries = near_list.shape[1]
    anywhere = pl.BlockSpec(memory_space=pl.ANY)
    return pl.pallas_call(
        main_kernel,
        out_shape=jax.ShapeDtypeStruct((3, PTS), F32),
        in_specs=[anywhere] * 5,
        out_specs=pl.BlockSpec(memory_space=pltpu.VMEM),
        scratch_shapes=[
            pltpu.VMEM((3, PTS), F32),
            pltpu.VMEM((3, PTS), F32),
            pltpu.VMEM(upsample.shape, F32),
            pltpu.VMEM((1, PEERS), jnp.int32),
            pltpu.VMEM((2, entries), jnp.int32),
            pltpu.VMEM((PEERS, 128), jnp.int32),
            pltpu.SMEM((PEERS, 128), jnp.int32),
            pltpu.VMEM((PANELS + 1, 8, 128), F32),
            pltpu.VMEM((PEERS, 8, 128), F32),
            pltpu.VMEM((128, PTS), F32),
            pltpu.VMEM((8, PTS), F32),
            pltpu.VMEM((PEERS - 1, 8, 128), F32),
            pltpu.VMEM((BLOCKS, 8, PTS), F32),
            pltpu.VMEM((2, 48, PTS), BF16),
            pltpu.VMEM((2, 16, PTS), F32),
        ]
        + [pltpu.VMEM((48, PTS), BF16)] * 2
        + [pltpu.VMEM((48, PTS), BF16)] * 4
        + [pltpu.VMEM((PTS, PTS), F32)] * 2
        + [pltpu.VMEM((2 * PTS, PTS), BF16)] * 2
        + [pltpu.SemaphoreType.DMA((5,))]
        + [pltpu.SemaphoreType.DMA((PEERS - 1,))] * 2
        + [pltpu.SemaphoreType.DMA((COLUMN,))] * 2,
        compiler_params=pltpu.CompilerParams(
            collective_id=0, has_side_effects=True, vmem_limit_bytes=62 << 20
        ),
    )(positions, density, upsample, cell_map, jnp.transpose(near_list, (0, 2, 1)).reshape(2, entries))


def solution(mesh):
    placed = (
        P(None, ("blk", "nbr")),
        P(None, ("blk", "nbr")),
        P(),
        P("blk", None),
        P(("blk", "nbr"), None, None),
    )
    return jax.shard_map(
        shards, mesh=mesh, in_specs=placed, out_specs=P(None, ("blk", "nbr")), check_vma=False
    )
```

```python
import functools
import math

import jax
import jax.numpy as jnp
from jax import lax
from jax.experimental import pallas as pl
from jax.experimental.pallas import tpu as pltpu
from jax.sharding import PartitionSpec as P

F32 = jnp.float32
BF16 = jnp.bfloat16
MESH = pl.DeviceIdType.MESH
FAR_REG_SQ = 0.0625
NEAR_REG_SQ = 0.01
STOKES_COEF = 1.0 / (8.0 * math.pi)

PTS = 512
PANELS = 16
SLOTS = 4
PEERS = 32
ZN = 4
YN = 8
XN = 4
NEAR_FIRST = 8
COLUMN = ZN * YN
FAR0 = PEERS - 1
BLOCKS = FAR0 + COLUMN
CHUNK = 64


def split3(a):
    a1 = a.astype(BF16)
    r = a - a1.astype(F32)
    a2 = r.astype(BF16)
    r = r - a2.astype(F32)
    return a1, a2, r.astype(BF16)


def split3f(a):
    a1 = a.astype(BF16).astype(F32)
    r = a - a1
    a2 = r.astype(BF16).astype(F32)
    return a1, a2, r - a2


def bc(t, r):
    return jnp.broadcast_to(t[r : r + 1, :], t.shape)


def prepare(t, center, row, ya_ref, w_ref):
    tc = t - center
    g = pltpu.roll(tc, 4, 0)
    sq = tc * tc
    df = tc * g
    nb = jnp.broadcast_to(sq[0:1] + sq[1:2] + sq[2:3], t.shape)
    db = jnp.broadcast_to(df[0:1] + df[1:2] + df[2:3], t.shape)
    s = jnp.where(row < 3, tc, jnp.where(row == 3, nb, jnp.where(row == 4, 1.0, 0.0)))
    s1, s2, s3 = split3f(s)
    ya_ref[...] = jnp.concatenate([s1, s2, s3, s1, s2, s1], axis=0).astype(BF16)
    low = row < 4
    f2 = jnp.where(low, g, tc)
    w1 = jnp.where(low, bc(tc, 0), bc(tc, 1)) * f2
    w2 = jnp.where(low, bc(tc, 2) * g, nb * tc + db * g)
    w1 = jnp.where(row == 3, bc(tc, 4), jnp.where(row == 7, bc(tc, 5), w1))
    w2 = jnp.where(row == 3, bc(tc, 6), w2)
    p1, p2, p3 = split3(jnp.concatenate([w1, w2], axis=0))
    w_ref[0:16, :] = p1
    w_ref[16:32, :] = p2
    w_ref[32:48, :] = p3


def target_rows(x, reg_sq):
    n = x[0] * x[0] + x[1] * x[1] + x[2] * x[2]
    one = jnp.ones_like(n)
    z = jnp.zeros_like(n)
    t = jnp.concatenate([-2.0 * x[0], -2.0 * x[1], -2.0 * x[2], one, n + reg_sq, z, z, z], axis=0)
    t1, t2, t3 = split3f(t)
    return jnp.concatenate([t1, t1, t1, t2, t2, t3], axis=0).astype(BF16), n


def distances(ya_ref, r, n, xa, d_ref):
    d_ref[r : r + n, :] = lax.dot_general(
        ya_ref[:, r : r + n], xa, (((0,), (0,)), ((), ())), preferred_element_type=F32
    )


def weights(d_ref, r, n, b_ref):
    s = lax.rsqrt(d_ref[r : r + n, :])
    b = s * (s * s)
    hi = b.astype(BF16)
    b_ref[r : r + n, :] = hi
    b_ref[PTS + r : PTS + r + n, :] = (b - hi.astype(F32)).astype(BF16)


def contract_hi(w_ref, b_ref):
    p = jnp.dot(w_ref[...], b_ref[0:PTS, :], preferred_element_type=F32)
    return p[:16] + p[16:32] + p[32:]


def contract_lo(w_ref, b_ref):
    p = jnp.dot(w_ref[0:32, :], b_ref[PTS : 2 * PTS, :], preferred_element_type=F32)
    return p[:16] + p[16:]


def combine(acc, x, n, reg_sq):
    f = [acc[3:4], acc[7:8], acc[11:12]]
    yf = [[acc[4 * b + a : 4 * b + a + 1] for a in range(3)] for b in range(3)]
    z = [acc[12 + a : 13 + a] for a in range(3)]
    xf = x[0] * f[0] + x[1] * f[1] + x[2] * f[2] - (yf[0][0] + yf[1][1] + yf[2][2])
    out = []
    for a in range(3):
        t = (2 * reg_sq + n) * f[a] + z[a]
        for b in range(3):
            t = t - x[b] * (2.0 * yf[b][a] + yf[a][b])
        out.append(t + x[a] * xf)
    return out


def upsampled(tiles, up):
    a1, a2, a3 = split3(tiles.reshape(-1, 128))
    u1, u2, u3 = up
    dot = functools.partial(jnp.dot, preferred_element_type=F32)
    fine = dot(a1, u1) + (dot(a1, u2) + dot(a2, u1)) + (dot(a1, u3) + dot(a2, u2) + dot(a3, u1))
    return fine.reshape(-1, 8, PTS)


def main_kernel(
    pos_hbm, den_hbm, up_hbm, map_hbm, list_hbm, out_ref,
    pos_ref, den_ref, up_ref, map_ref, list_ref, ids_ref, ids_smem, table, tiles, wide,
    own_ref, coarse, big, xa_ref, acc_ref, ya0, ya1, w0, w1, w2, w3, d0, d1, b0, b1,
    load_sem, near_send, near_recv, far_send, far_recv,
):
    blk = lax.axis_index("blk")
    nbr = lax.axis_index("nbr")
    zh = lax.div(blk, YN)
    y = lax.rem(blk, YN)
    zl = lax.div(nbr, 2 * XN)
    xc = lax.rem(lax.div(nbr, 2), XN)
    core = lax.rem(nbr, 2)

    def column(dz, dy):
        return (lax.rem(zh + dz, ZN) * YN + lax.rem(y + dy, YN), nbr)

    def row_index(o):
        dz = lax.div(o, 2 * XN)
        dx = lax.rem(lax.div(o, 2), XN)
        dc = lax.rem(o, 2)
        return (lax.rem(zl + dz, ZN) * XN + lax.rem(xc + dx, XN)) * 2 + lax.rem(core + dc, 2)

    def far_copy(src, dz, dy, hop_z, hop_y):
        f = dz * YN + dy
        return pltpu.make_async_remote_copy(
            src_ref=src, dst_ref=big.at[FAR0 + f], send_sem=far_send, recv_sem=far_recv.at[f],
            device_id=column(hop_z, hop_y), device_id_type=MESH,
        )

    def near_copy(o, group):
        return pltpu.make_async_remote_copy(
            src_ref=tiles.at[o], dst_ref=coarse.at[o - 1],
            send_sem=near_send, recv_sem=near_recv.at[group],
            device_id=(blk, row_index(o)), device_id_type=MESH,
        )

    def near_all(first, end, group):
        return pltpu.make_async_remote_copy(
            src_ref=tiles.at[first:end], dst_ref=coarse.at[first - 1 : end - 1],
            send_sem=near_send, recv_sem=near_recv.at[group],
            device_id=(blk, row_index(jnp.int32(1))), device_id_type=MESH,
        )

    loads = [
        pltpu.make_async_copy(src, dst, load_sem.at[q])
        for q, (src, dst) in enumerate(
            ((list_hbm, list_ref), (map_hbm, map_ref), (pos_hbm, pos_ref), (den_hbm, den_ref), (up_hbm, up_ref))
        )
    ]
    for load in loads:
        load.start()
    barrier = pltpu.get_barrier_semaphore()
    for dz in (1, ZN - 1):
        pl.semaphore_signal(barrier, inc=1, device_id=column(dz, 0), device_id_type=MESH)

    def greet_row(o, c):
        pl.semaphore_signal(barrier, inc=1, device_id=(blk, row_index(PEERS - o)), device_id_type=MESH)
        return c

    def greet_column(o, c):
        pl.semaphore_signal(barrier, inc=1, device_id=column(0, o), device_id_type=MESH)
        return c

    lax.fori_loop(1, PEERS, greet_row, 0)
    lax.fori_loop(1, YN, greet_column, 0)
    for load in loads:
        load.wait()

    peer_row = lax.broadcasted_iota(jnp.int32, (PEERS, PEERS), 0)
    place = jnp.where(peer_row == map_ref[...], 1.0, 0.0).astype(BF16)
    entries = list_ref.shape[1]
    ids = list_ref[...]
    panel = ids[0:1, :]
    target = ids[1:2, :]
    cell = lax.broadcasted_iota(jnp.int32, (PEERS, entries), 0)
    named = jnp.where(cell == target, 1.0, 0.0).astype(BF16)
    hit = jnp.dot(place, named, preferred_element_type=F32)
    before = jnp.where(
        lax.broadcasted_iota(jnp.int32, (entries, entries), 0) < lax.broadcasted_iota(jnp.int32, (entries, entries), 1),
        1.0, 0.0,
    ).astype(BF16)
    rank = jnp.dot(hit.astype(BF16), before, preferred_element_type=F32)
    number = (panel + 1).astype(F32)
    lane = lax.broadcasted_iota(jnp.int32, (PEERS, 128), 1)
    chosen = jnp.zeros((PEERS, 128), F32)
    for s in range(SLOTS):
        value = jnp.sum(jnp.where((hit > 0.5) & (rank == s), number, 0.0), axis=1, keepdims=True)
        chosen = jnp.where(lane == s, value, chosen)
    k = chosen.astype(jnp.int32) - 1
    quarter = jnp.bitwise_and(lane - k, 3)
    ids_ref[...] = jnp.where(k < 0, PANELS, jnp.bitwise_and(k, PANELS - 4) + quarter)
    to_smem = pltpu.make_async_copy(ids_ref, ids_smem, load_sem.at[0])
    to_smem.start()

    zero = jnp.zeros((1, PTS), F32)
    own = jnp.concatenate([pos_ref[...], zero, den_ref[...], zero], axis=0)
    own_ref[...] = own
    big[FAR0] = own
    upper = lax.broadcasted_iota(jnp.int32, (8, 128), 0) < 4
    for v in range(4):
        part = own[:, 128 * v : 128 * v + 128]
        part = jnp.where(upper, part, 0.25 * part)
        for r in range(4):
            table[4 * v + r] = part if r == 0 else pltpu.roll(part, 32 * r, 1)
    table[PANELS] = jnp.zeros((8, 128), F32)
    lane_slot = lax.broadcasted_iota(jnp.int32, (8, 128), 1) // 32
    to_smem.wait()

    def route(o):
        peer = row_index(o)
        tile = jnp.zeros((8, 128), F32)
        for s in range(SLOTS):
            at = jnp.minimum(jnp.maximum(ids_smem[peer, s], 0), PANELS)
            tile = jnp.where(lane_slot == s, table[at], tile)
        tiles[o] = tile

    def route_four(i, c):
        for u in range(4):
            route(4 * i + u)
        return c

    lax.fori_loop(0, PEERS // 4, route_four, 0)

    pl.semaphore_wait(barrier, 2 + (YN - 1) + (PEERS - 1))
    far_copy(own_ref, 1, 0, 1, 0).start()
    far_copy(own_ref, 3, 0, 3, 0).start()

    def send_near(group):
        def send(o, c):
            near_copy(o, group).start()
            return c

        return send

    def send_own(o, c):
        far_copy(own_ref, 0, o, 0, o).start()
        return c

    def fan(dz):
        def send(o, c):
            far_copy(big.at[FAR0 + dz * YN], dz, o, 0, o).start()
            return c

        return send

    lax.fori_loop(1, NEAR_FIRST, send_near(0), 0)
    lax.fori_loop(1, YN, send_own, 0)
    lax.fori_loop(NEAR_FIRST, PEERS, send_near(1), 0)

    up = up_ref[...]
    none = jnp.zeros_like(up)
    for s in range(SLOTS):
        wide[32 * s : 32 * s + 32, :] = jnp.concatenate([up if q == s else none for q in range(SLOTS)], axis=1)
    z1 = jnp.zeros((1, 1), F32)
    means = [jnp.mean(own[i : i + 1], axis=1, keepdims=True) for i in range(3)]
    center = jnp.concatenate(means + [z1] * 5, axis=0)
    x = [own[i : i + 1] - means[i] for i in range(3)]
    xa_ref[0], n = target_rows(x, NEAR_REG_SQ)
    xa_ref[1], _ = target_rows(x, FAR_REG_SQ)
    acc_ref[...] = jnp.zeros_like(acc_ref)
    b1[...] = jnp.zeros_like(b1)
    w3[...] = jnp.zeros_like(w3)
    row = lax.broadcasted_iota(jnp.int32, (8, PTS), 0)

    ya = (ya0, ya1)
    w = (w0, w1, w2, w3)
    d = (d0, d1)
    b = (b0, b1)

    def block(i):
        late = jnp.where(i < 47, i, jnp.where(i < 55, i + 8, i - 8))
        far = jnp.where(i == 0, FAR0, jnp.where(i < 15, FAR0 - 7 + i, late))
        return jnp.where(kind(i) == 1, far, jnp.where(i < 15, i - 1, i - 8))

    def kind(i):
        return jnp.where(i == 0, 1, jnp.where(i < 8, 0, jnp.where(i < 15, 1, jnp.where(i < 39, 0, 1))))

    def prep(i, j):
        prepare(big[block(i)], center, row, ya[j % 2], w[j % 4])

    def step(i, j, more=2):
        p = j % 2
        q = 1 - p
        half = PTS // 2
        xa = xa_ref[kind(i + 1)]
        before_kind = kind(i - 1)
        before_w = w[(j - 1) % 4]
        acc_ref[before_kind] += contract_hi(before_w, b[q])
        if more > 0:
            distances(ya[q], 0, half, xa, d[q])
        for r in range(4):
            weights(d[p], CHUNK * r, CHUNK, b[p])
        acc_ref[before_kind] += contract_lo(before_w, b[q])
        if more > 0:
            distances(ya[q], half, half, xa, d[q])
        for r in range(4, 8):
            weights(d[p], CHUNK * r, CHUNK, b[p])
        if more > 1:
            prep(i + 2, j + 2)

    prep(0, 0)
    distances(ya0, 0, PTS, xa_ref[1], d0)
    near_all(1, NEAR_FIRST, 0).wait_recv()
    fine = functools.partial(upsampled, up=split3(wide[...]))
    big[0 : NEAR_FIRST - 1] = fine(coarse[0 : NEAR_FIRST - 1])
    prep(1, 1)

    def take_far(i):
        f = block(i) - FAR0

        @pl.when((kind(i) == 1) & (lax.rem(f, YN) != 0))
        def _():
            far_copy(own_ref, 0, f, 0, 1).wait_recv()

    def body(k, c):
        @pl.when(k == 2)
        def _():
            far_copy(own_ref, 1, 0, 1, 0).wait_recv()
            far_copy(big.at[FAR0 + YN], 2, 0, 1, 0).start()
            lax.fori_loop(1, YN, fan(1), 0)
            far_copy(own_ref, 3, 0, 3, 0).wait_recv()
            lax.fori_loop(1, YN, fan(3), 0)

        @pl.when(k == 3)
        def _():
            near_all(NEAR_FIRST, PEERS, 1).wait_recv()
            big[NEAR_FIRST - 1 : FAR0] = fine(coarse[NEAR_FIRST - 1 : FAR0])

        @pl.when(k == 5)
        def _():
            far_copy(big.at[FAR0 + YN], 2, 0, 1, 0).wait_recv()
            lax.fori_loop(1, YN, fan(2), 0)

        for j in range(4):
            take_far(4 * k + j + 2)
        for j in range(4):
            step(4 * k + j, j)
        return c

    lax.fori_loop(0, 15, body, 0)
    take_far(BLOCKS - 1)
    step(BLOCKS - 3, 0)
    step(BLOCKS - 2, 1, more=1)
    step(BLOCKS - 1, 2, more=0)
    acc_ref[1] += contract_hi(w2, b0) + contract_lo(w2, b0)

    near = combine(acc_ref[0], x, n, NEAR_REG_SQ)
    far = combine(acc_ref[1], x, n, FAR_REG_SQ)
    for a in range(3):
        out_ref[a : a + 1, :] = STOKES_COEF * (far[a] + near[a])

    near_all(1, PEERS, 0).wait_send()
    pltpu.make_async_remote_copy(
        src_ref=big.at[FAR0 + 1 : BLOCKS], dst_ref=big.at[FAR0 + 1 : BLOCKS],
        send_sem=far_send, recv_sem=far_recv.at[0],
        device_id=column(1, 0), device_id_type=MESH,
    ).wait_send()


def shards(positions, density, upsample, cell_map, near_list):
    entries = near_list.shape[1]
    anywhere = pl.BlockSpec(memory_space=pl.ANY)
    return pl.pallas_call(
        main_kernel,
        out_shape=jax.ShapeDtypeStruct((3, PTS), F32),
        in_specs=[anywhere] * 5,
        out_specs=pl.BlockSpec(memory_space=pltpu.VMEM),
        scratch_shapes=[
            pltpu.VMEM((3, PTS), F32),
            pltpu.VMEM((3, PTS), F32),
            pltpu.VMEM(upsample.shape, F32),
            pltpu.VMEM((1, PEERS), jnp.int32),
            pltpu.VMEM((2, entries), jnp.int32),
            pltpu.VMEM((PEERS, 128), jnp.int32),
            pltpu.SMEM((PEERS, 128), jnp.int32),
            pltpu.VMEM((PANELS + 1, 8, 128), F32),
            pltpu.VMEM((PEERS, 8, 128), F32),
            pltpu.VMEM((128, PTS), F32),
            pltpu.VMEM((8, PTS), F32),
            pltpu.VMEM((PEERS - 1, 8, 128), F32),
            pltpu.VMEM((BLOCKS, 8, PTS), F32),
            pltpu.VMEM((2, 48, PTS), BF16),
            pltpu.VMEM((2, 16, PTS), F32),
        ]
        + [pltpu.VMEM((48, PTS), BF16)] * 2
        + [pltpu.VMEM((48, PTS), BF16)] * 4
        + [pltpu.VMEM((PTS, PTS), F32)] * 2
        + [pltpu.VMEM((2 * PTS, PTS), BF16)] * 2
        + [pltpu.SemaphoreType.DMA((5,))]
        + [pltpu.SemaphoreType.DMA, pltpu.SemaphoreType.DMA((2,))]
        + [pltpu.SemaphoreType.DMA, pltpu.SemaphoreType.DMA((COLUMN,))],
        compiler_params=pltpu.CompilerParams(
            collective_id=0, has_side_effects=True, vmem_limit_bytes=62 << 20
        ),
    )(positions, density, upsample, cell_map, jnp.transpose(near_list, (0, 2, 1)).reshape(2, entries))


def solution(mesh):
    placed = (
        P(None, ("blk", "nbr")),
        P(None, ("blk", "nbr")),
        P(),
        P("blk", None),
        P(("blk", "nbr"), None, None),
    )
    return jax.shard_map(
        shards, mesh=mesh, in_specs=placed, out_specs=P(None, ("blk", "nbr")), check_vma=False
    )
```

```python
import functools
import math

import jax
import jax.numpy as jnp
from jax import lax
from jax.experimental import pallas as pl
from jax.experimental.pallas import tpu as pltpu
from jax.sharding import PartitionSpec as P

F32 = jnp.float32
BF16 = jnp.bfloat16
MESH = pl.DeviceIdType.MESH
FAR_REG_SQ = 0.0625
NEAR_REG_SQ = 0.01
STOKES_COEF = 1.0 / (8.0 * math.pi)

PTS = 512
PANELS = 16
SLOTS = 4
PEERS = 32
ZN = 4
YN = 8
XN = 4
NEAR_FIRST = 8
COLUMN = ZN * YN
FAR0 = PEERS - 1
BLOCKS = FAR0 + COLUMN
CHUNK = 64


def split3(a):
    a1 = a.astype(BF16)
    r = a - a1.astype(F32)
    a2 = r.astype(BF16)
    r = r - a2.astype(F32)
    return a1, a2, r.astype(BF16)


def split3f(a):
    a1 = a.astype(BF16).astype(F32)
    r = a - a1
    a2 = r.astype(BF16).astype(F32)
    return a1, a2, r - a2


def bc(t, r):
    return jnp.broadcast_to(t[r : r + 1, :], t.shape)


def prepare(t, center, row, ya_ref, w_ref):
    tc = t - center
    g = pltpu.roll(tc, 4, 0)
    sq = tc * tc
    df = tc * g
    nb = jnp.broadcast_to(sq[0:1] + sq[1:2] + sq[2:3], t.shape)
    db = jnp.broadcast_to(df[0:1] + df[1:2] + df[2:3], t.shape)
    s = jnp.where(row < 3, tc, jnp.where(row == 3, nb, jnp.where(row == 4, 1.0, 0.0)))
    s1, s2, s3 = split3f(s)
    ya_ref[...] = jnp.concatenate([s1, s2, s3, s1, s2, s1], axis=0).astype(BF16)
    low = row < 4
    f2 = jnp.where(low, g, tc)
    w1 = jnp.where(low, bc(tc, 0), bc(tc, 1)) * f2
    w2 = jnp.where(low, bc(tc, 2) * g, nb * tc + db * g)
    w1 = jnp.where(row == 3, bc(tc, 4), jnp.where(row == 7, bc(tc, 5), w1))
    w2 = jnp.where(row == 3, bc(tc, 6), w2)
    p1, p2, p3 = split3(jnp.concatenate([w1, w2], axis=0))
    w_ref[0:16, :] = p1
    w_ref[16:32, :] = p2
    w_ref[32:48, :] = p3


def target_rows(x, reg_sq):
    n = x[0] * x[0] + x[1] * x[1] + x[2] * x[2]
    one = jnp.ones_like(n)
    z = jnp.zeros_like(n)
    t = jnp.concatenate([-2.0 * x[0], -2.0 * x[1], -2.0 * x[2], one, n + reg_sq, z, z, z], axis=0)
    t1, t2, t3 = split3f(t)
    return jnp.concatenate([t1, t1, t1, t2, t2, t3], axis=0).astype(BF16), n


def distances(ya_ref, r, n, xa, d_ref):
    d_ref[r : r + n, :] = lax.dot_general(
        ya_ref[:, r : r + n], xa, (((0,), (0,)), ((), ())), preferred_element_type=F32
    )


def weights(d_ref, r, n, b_ref):
    s = lax.rsqrt(d_ref[r : r + n, :])
    b = s * (s * s)
    hi = b.astype(BF16)
    b_ref[r : r + n, :] = hi
    b_ref[PTS + r : PTS + r + n, :] = (b - hi.astype(F32)).astype(BF16)


def contract_hi(w_ref, b_ref):
    p = jnp.dot(w_ref[...], b_ref[0:PTS, :], preferred_element_type=F32)
    return p[:16] + p[16:32] + p[32:]


def contract_lo(w_ref, b_ref):
    p = jnp.dot(w_ref[0:32, :], b_ref[PTS : 2 * PTS, :], preferred_element_type=F32)
    return p[:16] + p[16:]


def combine(acc, x, n, reg_sq):
    f = [acc[3:4], acc[7:8], acc[11:12]]
    yf = [[acc[4 * b + a : 4 * b + a + 1] for a in range(3)] for b in range(3)]
    z = [acc[12 + a : 13 + a] for a in range(3)]
    xf = x[0] * f[0] + x[1] * f[1] + x[2] * f[2] - (yf[0][0] + yf[1][1] + yf[2][2])
    out = []
    for a in range(3):
        t = (2 * reg_sq + n) * f[a] + z[a]
        for b in range(3):
            t = t - x[b] * (2.0 * yf[b][a] + yf[a][b])
        out.append(t + x[a] * xf)
    return out


def upsampled(tiles, up):
    a1, a2, a3 = split3(tiles.reshape(-1, 128))
    u1, u2, u3 = up
    dot = functools.partial(jnp.dot, preferred_element_type=F32)
    fine = dot(a1, u1) + (dot(a1, u2) + dot(a2, u1)) + (dot(a1, u3) + dot(a2, u2) + dot(a3, u1))
    return fine.reshape(-1, 8, PTS)


def main_kernel(
    pos_hbm, den_hbm, up_hbm, map_hbm, list_hbm, out_ref,
    pos_ref, den_ref, up_ref, map_ref, list_ref, ids_ref, ids_smem, table, tiles, wide,
    own_ref, coarse, big, xa_ref, acc_ref, ya0, ya1, w0, w1, w2, w3, d0, d1, b0, b1,
    load_sem, near_send, near_recv, far_send, far_recv, fan_recv,
):
    blk = lax.axis_index("blk")
    nbr = lax.axis_index("nbr")
    zh = lax.div(blk, YN)
    y = lax.rem(blk, YN)
    zl = lax.div(nbr, 2 * XN)
    xc = lax.rem(lax.div(nbr, 2), XN)
    core = lax.rem(nbr, 2)

    def column(dz, dy):
        return (lax.rem(zh + dz, ZN) * YN + lax.rem(y + dy, YN), nbr)

    def row_index(o):
        dz = lax.div(o, 2 * XN)
        dx = lax.rem(lax.div(o, 2), XN)
        dc = lax.rem(o, 2)
        return (lax.rem(zl + dz, ZN) * XN + lax.rem(xc + dx, XN)) * 2 + lax.rem(core + dc, 2)

    def far_copy(src, dz, dy, hop_z, hop_y):
        f = dz * YN + dy
        return pltpu.make_async_remote_copy(
            src_ref=src, dst_ref=big.at[FAR0 + f], send_sem=far_send,
            recv_sem=fan_recv.at[dz] if hop_z == 0 else far_recv.at[dz],
            device_id=column(hop_z, hop_y), device_id_type=MESH,
        )

    def fan_all(dz):
        blocks = big.at[FAR0 + dz * YN + 1 : FAR0 + dz * YN + YN]
        return pltpu.make_async_remote_copy(
            src_ref=blocks, dst_ref=blocks, send_sem=far_send, recv_sem=fan_recv.at[dz],
            device_id=column(0, 1), device_id_type=MESH,
        )

    def near_copy(o, group):
        return pltpu.make_async_remote_copy(
            src_ref=tiles.at[o], dst_ref=coarse.at[o - 1],
            send_sem=near_send, recv_sem=near_recv.at[group],
            device_id=(blk, row_index(o)), device_id_type=MESH,
        )

    def near_all(first, end, group):
        return pltpu.make_async_remote_copy(
            src_ref=tiles.at[first:end], dst_ref=coarse.at[first - 1 : end - 1],
            send_sem=near_send, recv_sem=near_recv.at[group],
            device_id=(blk, row_index(jnp.int32(1))), device_id_type=MESH,
        )

    loads = [
        pltpu.make_async_copy(src, dst, load_sem.at[q])
        for q, (src, dst) in enumerate(
            ((list_hbm, list_ref), (map_hbm, map_ref), (pos_hbm, pos_ref), (den_hbm, den_ref), (up_hbm, up_ref))
        )
    ]
    for load in loads:
        load.start()
    barrier = pltpu.get_barrier_semaphore()
    for dz in (1, ZN - 1):
        pl.semaphore_signal(barrier, inc=1, device_id=column(dz, 0), device_id_type=MESH)

    def greet_row(o, c):
        pl.semaphore_signal(barrier, inc=1, device_id=(blk, row_index(PEERS - o)), device_id_type=MESH)
        return c

    def greet_column(o, c):
        pl.semaphore_signal(barrier, inc=1, device_id=column(0, o), device_id_type=MESH)
        return c

    lax.fori_loop(1, PEERS, greet_row, 0)
    lax.fori_loop(1, YN, greet_column, 0)
    for load in loads:
        load.wait()

    peer_row = lax.broadcasted_iota(jnp.int32, (PEERS, PEERS), 0)
    place = jnp.where(peer_row == map_ref[...], 1.0, 0.0).astype(BF16)
    entries = list_ref.shape[1]
    ids = list_ref[...]
    panel = ids[0:1, :]
    target = ids[1:2, :]
    cell = lax.broadcasted_iota(jnp.int32, (PEERS, entries), 0)
    named = jnp.where(cell == target, 1.0, 0.0).astype(BF16)
    hit = jnp.dot(place, named, preferred_element_type=F32)
    before = jnp.where(
        lax.broadcasted_iota(jnp.int32, (entries, entries), 0) < lax.broadcasted_iota(jnp.int32, (entries, entries), 1),
        1.0, 0.0,
    ).astype(BF16)
    rank = jnp.dot(hit.astype(BF16), before, preferred_element_type=F32)
    number = (panel + 1).astype(F32)
    lane = lax.broadcasted_iota(jnp.int32, (PEERS, 128), 1)
    chosen = jnp.zeros((PEERS, 128), F32)
    for s in range(SLOTS):
        value = jnp.sum(jnp.where((hit > 0.5) & (rank == s), number, 0.0), axis=1, keepdims=True)
        chosen = jnp.where(lane == s, value, chosen)
    k = chosen.astype(jnp.int32) - 1
    quarter = jnp.bitwise_and(lane - k, 3)
    ids_ref[...] = jnp.where(k < 0, PANELS, jnp.bitwise_and(k, PANELS - 4) + quarter)
    to_smem = pltpu.make_async_copy(ids_ref, ids_smem, load_sem.at[0])
    to_smem.start()

    zero = jnp.zeros((1, PTS), F32)
    own = jnp.concatenate([pos_ref[...], zero, den_ref[...], zero], axis=0)
    own_ref[...] = own
    big[FAR0] = own
    upper = lax.broadcasted_iota(jnp.int32, (8, 128), 0) < 4
    for v in range(4):
        part = own[:, 128 * v : 128 * v + 128]
        part = jnp.where(upper, part, 0.25 * part)
        for r in range(4):
            table[4 * v + r] = part if r == 0 else pltpu.roll(part, 32 * r, 1)
    table[PANELS] = jnp.zeros((8, 128), F32)
    lane_slot = lax.broadcasted_iota(jnp.int32, (8, 128), 1) // 32
    to_smem.wait()

    def route(o):
        peer = row_index(o)
        tile = jnp.zeros((8, 128), F32)
        for s in range(SLOTS):
            at = jnp.minimum(jnp.maximum(ids_smem[peer, s], 0), PANELS)
            tile = jnp.where(lane_slot == s, table[at], tile)
        tiles[o] = tile

    def route_four(i, c):
        for u in range(4):
            route(4 * i + u)
        return c

    lax.fori_loop(0, PEERS // 4, route_four, 0)

    pl.semaphore_wait(barrier, 2 + (YN - 1) + (PEERS - 1))
    far_copy(own_ref, 1, 0, 1, 0).start()
    far_copy(own_ref, 3, 0, 3, 0).start()

    def send_near(group):
        def send(o, c):
            near_copy(o, group).start()
            return c

        return send

    def send_own(o, c):
        far_copy(own_ref, 0, o, 0, o).start()
        return c

    def fan(dz):
        def send(o, c):
            far_copy(big.at[FAR0 + dz * YN], dz, o, 0, o).start()
            return c

        return send

    lax.fori_loop(1, NEAR_FIRST, send_near(0), 0)
    lax.fori_loop(1, YN, send_own, 0)
    lax.fori_loop(NEAR_FIRST, PEERS, send_near(1), 0)

    up = up_ref[...]
    none = jnp.zeros_like(up)
    for s in range(SLOTS):
        wide[32 * s : 32 * s + 32, :] = jnp.concatenate([up if q == s else none for q in range(SLOTS)], axis=1)
    z1 = jnp.zeros((1, 1), F32)
    means = [jnp.mean(own[i : i + 1], axis=1, keepdims=True) for i in range(3)]
    center = jnp.concatenate(means + [z1] * 5, axis=0)
    x = [own[i : i + 1] - means[i] for i in range(3)]
    xa_ref[0], n = target_rows(x, NEAR_REG_SQ)
    xa_ref[1], _ = target_rows(x, FAR_REG_SQ)
    acc_ref[...] = jnp.zeros_like(acc_ref)
    b1[...] = jnp.zeros_like(b1)
    w3[...] = jnp.zeros_like(w3)
    row = lax.broadcasted_iota(jnp.int32, (8, PTS), 0)

    ya = (ya0, ya1)
    w = (w0, w1, w2, w3)
    d = (d0, d1)
    b = (b0, b1)

    def block(i):
        late = jnp.where(i < 47, i, jnp.where(i < 55, i + 8, i - 8))
        far = jnp.where(i == 0, FAR0, jnp.where(i < 15, FAR0 - 7 + i, late))
        return jnp.where(kind(i) == 1, far, jnp.where(i < 15, i - 1, i - 8))

    def kind(i):
        return jnp.where(i == 0, 1, jnp.where(i < 8, 0, jnp.where(i < 15, 1, jnp.where(i < 39, 0, 1))))

    def prep(i, j):
        prepare(big[block(i)], center, row, ya[j % 2], w[j % 4])

    def step(i, j, more=2):
        p = j % 2
        q = 1 - p
        half = PTS // 2
        xa = xa_ref[kind(i + 1)]
        before_kind = kind(i - 1)
        before_w = w[(j - 1) % 4]
        acc_ref[before_kind] += contract_hi(before_w, b[q])
        if more > 0:
            distances(ya[q], 0, half, xa, d[q])
        for r in range(4):
            weights(d[p], CHUNK * r, CHUNK, b[p])
        acc_ref[before_kind] += contract_lo(before_w, b[q])
        if more > 0:
            distances(ya[q], half, half, xa, d[q])
        for r in range(4, 8):
            weights(d[p], CHUNK * r, CHUNK, b[p])
        if more > 1:
            prep(i + 2, j + 2)

    prep(0, 0)
    distances(ya0, 0, PTS, xa_ref[1], d0)
    near_all(1, NEAR_FIRST, 0).wait_recv()
    fine = functools.partial(upsampled, up=split3(wide[...]))
    big[0 : NEAR_FIRST - 1] = fine(coarse[0 : NEAR_FIRST - 1])
    prep(1, 1)

    def first_body(k, c):
        @pl.when(k == 1)
        def _():
            fan_all(0).wait_recv()

        @pl.when(k == 2)
        def _():
            far_copy(own_ref, 1, 0, 1, 0).wait_recv()
            far_copy(big.at[FAR0 + YN], 2, 0, 1, 0).start()
            lax.fori_loop(1, YN, fan(1), 0)
            far_copy(own_ref, 3, 0, 3, 0).wait_recv()
            lax.fori_loop(1, YN, fan(3), 0)

        for j in range(4):
            step(4 * k + j, j)
        return c

    def body(k, c):
        @pl.when(k == 0)
        def _():
            near_all(NEAR_FIRST, PEERS, 1).wait_recv()
            big[NEAR_FIRST - 1 : FAR0] = fine(coarse[NEAR_FIRST - 1 : FAR0])

        @pl.when(k == 1)
        def _():
            far_copy(big.at[FAR0 + YN], 2, 0, 1, 0).wait_recv()
            lax.fori_loop(1, YN, fan(2), 0)

        @pl.when(k == 2)
        def _():
            fan_all(1).wait_recv()
            fan_all(3).wait_recv()

        @pl.when(k == 3)
        def _():
            fan_all(2).wait_recv()

        for j in range(12):
            step(12 * k + 12 + j, j % 4)
        return c

    lax.fori_loop(0, 3, first_body, 0)
    lax.fori_loop(0, 4, body, 0)
    step(BLOCKS - 3, 0)
    step(BLOCKS - 2, 1, more=1)
    step(BLOCKS - 1, 2, more=0)
    acc_ref[1] += contract_hi(w2, b0) + contract_lo(w2, b0)

    near = combine(acc_ref[0], x, n, NEAR_REG_SQ)
    far = combine(acc_ref[1], x, n, FAR_REG_SQ)
    for a in range(3):
        out_ref[a : a + 1, :] = STOKES_COEF * (far[a] + near[a])

    near_all(1, PEERS, 0).wait_send()
    pltpu.make_async_remote_copy(
        src_ref=big.at[FAR0 + 1 : BLOCKS], dst_ref=big.at[FAR0 + 1 : BLOCKS],
        send_sem=far_send, recv_sem=far_recv.at[1],
        device_id=column(1, 0), device_id_type=MESH,
    ).wait_send()


def shards(positions, density, upsample, cell_map, near_list):
    entries = near_list.shape[1]
    anywhere = pl.BlockSpec(memory_space=pl.ANY)
    return pl.pallas_call(
        main_kernel,
        out_shape=jax.ShapeDtypeStruct((3, PTS), F32),
        in_specs=[anywhere] * 5,
        out_specs=pl.BlockSpec(memory_space=pltpu.VMEM),
        scratch_shapes=[
            pltpu.VMEM((3, PTS), F32),
            pltpu.VMEM((3, PTS), F32),
            pltpu.VMEM(upsample.shape, F32),
            pltpu.VMEM((1, PEERS), jnp.int32),
            pltpu.VMEM((2, entries), jnp.int32),
            pltpu.VMEM((PEERS, 128), jnp.int32),
            pltpu.SMEM((PEERS, 128), jnp.int32),
            pltpu.VMEM((PANELS + 1, 8, 128), F32),
            pltpu.VMEM((PEERS, 8, 128), F32),
            pltpu.VMEM((128, PTS), F32),
            pltpu.VMEM((8, PTS), F32),
            pltpu.VMEM((PEERS - 1, 8, 128), F32),
            pltpu.VMEM((BLOCKS, 8, PTS), F32),
            pltpu.VMEM((2, 48, PTS), BF16),
            pltpu.VMEM((2, 16, PTS), F32),
        ]
        + [pltpu.VMEM((48, PTS), BF16)] * 2
        + [pltpu.VMEM((48, PTS), BF16)] * 4
        + [pltpu.VMEM((PTS, PTS), F32)] * 2
        + [pltpu.VMEM((2 * PTS, PTS), BF16)] * 2
        + [pltpu.SemaphoreType.DMA((5,))]
        + [pltpu.SemaphoreType.DMA, pltpu.SemaphoreType.DMA((2,))]
        + [pltpu.SemaphoreType.DMA, pltpu.SemaphoreType.DMA((ZN,)), pltpu.SemaphoreType.DMA((ZN,))],
        compiler_params=pltpu.CompilerParams(
            collective_id=0, has_side_effects=True, vmem_limit_bytes=62 << 20
        ),
    )(positions, density, upsample, cell_map, jnp.transpose(near_list, (0, 2, 1)).reshape(2, entries))


def solution(mesh):
    placed = (
        P(None, ("blk", "nbr")),
        P(None, ("blk", "nbr")),
        P(),
        P("blk", None),
        P(("blk", "nbr"), None, None),
    )
    return jax.shard_map(
        shards, mesh=mesh, in_specs=placed, out_specs=P(None, ("blk", "nbr")), check_vma=False
    )
```
